32 devices in a mesh: pipe: 4 (over z), tile: 8 (over y, x, core).
Axes of the slice: x: 2, y: 2, z: 4, core: 2. Of those that a mesh axis runs over, the one named last changes fastest.
Arguments:
- x_next: bfloat16 [4, 1024, 8192], P('pipe', 'tile'), may hold values from -6 to 6
- x_saved: bfloat16 [4, 1024, 8192], P('pipe', 'tile'), may hold values from -6 to 6
- pending: bfloat16 [4, 1024, 8192], P('pipe', 'tile'), may hold values from -6 to 6
- gu_rows: int32 [4, 8, 1], P('pipe'), may hold values from 0 to 63, as said below
- gu_cols: int32 [4, 8, 1], P('pipe'), may hold values from 0 to 111
- gu_live: int32 [4, 8], P('pipe'), may hold values from 1 to 1, as said below
- down_rows: int32 [4, 8, 1], P('pipe'), may hold values from 0 to 111, as said below
- down_cols: int32 [4, 8, 1], P('pipe'), may hold values from 0 to 63
- down_live: int32 [4, 8], P('pipe'), may hold values from 1 to 1, as said below
- gate_up_tiles: bfloat16 [4, 8, 1, 2, 128, 128], P('pipe', 'tile'), may hold values from -0.5 to 0.5
- down_tiles: bfloat16 [4, 8, 1, 128, 128], P('pipe', 'tile'), may hold values from -0.5 to 0.5
Outputs:
- y_next: bfloat16 [4, 1024, 8192], P('pipe', 'tile')
- dx_saved: bfloat16 [4, 1024, 8192], P('pipe', 'tile')
- grad_gate_up: float32 [4, 8, 1, 2, 128, 128], P('pipe', 'tile')
- grad_down: float32 [4, 8, 1, 128, 128], P('pipe', 'tile')
The draws below stay inside these ranges and needn't reach their ends.
Inputs may be any that keep to these rules, and one draw needn't show every extreme that they name: Within a section the 8 x 1 slots of the gate and up lists name distinct tiles (gu_rows, gu_cols). Within a section the 8 x 1 slots of the down list name distinct tiles (down_rows, down_cols). `gu_live`: in every section some owner has all 1 slots live. `down_live`: in every section some owner has all 1 slots live.
All inputs are finite; a program needn't handle non-finite values.
Results may differ from the reference program's by a relative error of at most 0.0067.
Values may be sent and summed in bfloat16 or wider, within the bound.
A program may use at most 128 MiB of HBM per device.

```python
import jax
import jax.numpy as jnp

D = 8192
FF = 14336
BLOCK = 128
TILE_DEV = 1
SECTIONS = 4
OWNERS = 8
TOKENS = 1024


def tile_positions(key, salt, rows, cols):
    keys = jax.random.split(jax.random.fold_in(key, salt), SECTIONS)

    def one_section(section_key):
        return jax.random.permutation(section_key, rows * cols)[:OWNERS * TILE_DEV]
    positions = jax.vmap(one_section)(keys)
    return positions.reshape(SECTIONS, OWNERS, TILE_DEV).astype(jnp.int32)


def live_counts(key, salt):
    first_key, second_key = jax.random.split(jax.random.fold_in(key, salt))
    lowest = max(1, TILE_DEV // 4)
    counts = jax.random.randint(first_key, (SECTIONS, OWNERS), lowest, TILE_DEV + 1)
    fullest = jax.random.randint(second_key, (SECTIONS,), 0, OWNERS)
    owner_ids = jnp.arange(OWNERS, dtype=jnp.int32)
    return jnp.where(owner_ids[None, :] == fullest[:, None], TILE_DEV, counts).astype(jnp.int32)


def draw_gu_rows(key, part):
    return tile_positions(key, 11, D // BLOCK, FF // BLOCK) // (FF // BLOCK)


def draw_gu_cols(key, part):
    return tile_positions(key, 11, D // BLOCK, FF // BLOCK) % (FF // BLOCK)


def draw_down_rows(key, part):
    return tile_positions(key, 12, FF // BLOCK, D // BLOCK) // (D // BLOCK)


def draw_down_cols(key, part):
    return tile_positions(key, 12, FF // BLOCK, D // BLOCK) % (D // BLOCK)


def draw_gu_live(key, part):
    return live_counts(key, 21)


def draw_down_live(key, part):
    return live_counts(key, 22)


def block_scale(stream_key, extent, cuts, low, top_value):
    factor_of, own = 1.0, jax.random.fold_in(stream_key, 6)
    for axis_at, shards_of in cuts:
        heights = jnp.exp(jax.random.uniform(jax.random.fold_in(own, axis_at), (shards_of,), jnp.float32, low / len(cuts), top_value / len(cuts)))
        factor_of = factor_of * jnp.repeat(heights, extent[axis_at] // shards_of).reshape([-1 if axis == axis_at else 1 for axis in range(len(extent))])
    return factor_of


def bell_draw(rng, extent, deviation, most, cuts=(), kind=jnp.bfloat16):
    factor_of = block_scale(rng, extent, cuts, -0.22, 0.18) if cuts else 1.0
    result = jax.random.normal(rng, extent, jnp.float32) * deviation * factor_of
    return jnp.minimum(jnp.maximum(result, -most), most).astype(kind)


def setup_inputs(seed: int = 0) -> dict:
    streams_of = jax.random.split(jax.random.key(seed), 12)
    return {
        "x_next": bell_draw(streams_of[0], (SECTIONS, TOKENS, D), 1.0, 6.0, ((0, 4), (1, 8))),
        "x_saved": bell_draw(streams_of[1], (SECTIONS, TOKENS, D), 1.0, 6.0, ((0, 4), (1, 8))),
        "pending": bell_draw(streams_of[2], (SECTIONS, TOKENS, D), 1.0, 6.0, ((0, 4), (1, 8))),
        "gu_rows": draw_gu_rows(jax.random.fold_in(streams_of[11], 71), 0),
        "gu_cols": draw_gu_cols(jax.random.fold_in(streams_of[11], 71), 0),
        "gu_live": draw_gu_live(jax.random.fold_in(streams_of[11], 71), 0),
        "down_rows": draw_down_rows(jax.random.fold_in(streams_of[11], 71), 0),
        "down_cols": draw_down_cols(jax.random.fold_in(streams_of[11], 71), 0),
        "down_live": draw_down_live(jax.random.fold_in(streams_of[11], 71), 0),
        "gate_up_tiles": bell_draw(streams_of[9], (SECTIONS, OWNERS, TILE_DEV, 2, BLOCK, BLOCK), (max(BLOCK, BLOCK * OWNERS * TILE_DEV // (FF // BLOCK))) ** -0.5, 0.5, ((0, 4), (1, 8))),
        "down_tiles": bell_draw(streams_of[10], (SECTIONS, OWNERS, TILE_DEV, BLOCK, BLOCK), (max(BLOCK, BLOCK * OWNERS * TILE_DEV // (D // BLOCK))) ** -0.5, 0.5, ((0, 4), (1, 8))),
    }


def column_sum(parts, index, blocks):
    onehot = (index[:, None] == jnp.arange(blocks, dtype=jnp.int32)[None, :]).astype(jnp.float32)
    summed = jnp.einsum('tkq,kc->tcq', parts.astype(jnp.float32), onehot)
    return summed.reshape(parts.shape[0], blocks * parts.shape[2])


def one_section(x_next, x_saved, cot, gu_rows, gu_cols, gu_live, down_rows, down_cols, down_live, gate_up, down):
    count = OWNERS * TILE_DEV
    row_blocks = D // BLOCK
    col_blocks = FF // BLOCK
    g_rows = gu_rows.reshape(count)
    g_cols = gu_cols.reshape(count)
    d_rows = down_rows.reshape(count)
    d_cols = down_cols.reshape(count)
    slot_ids = jnp.arange(TILE_DEV, dtype=jnp.int32)
    g_live = (slot_ids[None, :] < gu_live[:, None]).reshape(count).astype(jnp.float32)
    d_live = (slot_ids[None, :] < down_live[:, None]).reshape(count).astype(jnp.float32)
    weights_gu = gate_up.reshape(count, 2, BLOCK, BLOCK).astype(jnp.float32)
    weights_down = down.reshape(count, BLOCK, BLOCK).astype(jnp.float32)

    def project(inputs):
        x_slots = inputs.reshape(TOKENS, row_blocks, BLOCK)[:, g_rows, :].astype(jnp.float32)
        parts = jnp.einsum('tkp,kgpq->gtkq', x_slots, weights_gu) * g_live[None, None, :, None]
        parts = parts.astype(jnp.bfloat16)
        return column_sum(parts[0], g_cols, col_blocks), column_sum(parts[1], g_cols, col_blocks), x_slots

    gate_next, up_next, unused = project(x_next)
    gate_saved, up_saved, x_slots = project(x_saved)
    sig_next = jax.nn.sigmoid(gate_next)
    hidden_next = (gate_next * sig_next * up_next).astype(jnp.bfloat16)
    sig = jax.nn.sigmoid(gate_saved)
    act = gate_saved * sig
    hidden_saved = (act * up_saved).astype(jnp.bfloat16)

    h_slots = hidden_next.reshape(TOKENS, col_blocks, BLOCK)[:, d_rows, :].astype(jnp.float32)
    y_part = (jnp.einsum('tkp,kpq->tkq', h_slots, weights_down) * d_live[None, :, None]).astype(jnp.bfloat16)
    y_next = column_sum(y_part, d_cols, row_blocks).astype(jnp.bfloat16)

    dy_slots = cot.reshape(TOKENS, row_blocks, BLOCK)[:, d_cols, :].astype(jnp.float32)
    hs_saved = hidden_saved.reshape(TOKENS, col_blocks, BLOCK)[:, d_rows, :].astype(jnp.float32)
    grad_down = jnp.einsum('tkp,tkq->kpq', hs_saved, dy_slots) * d_live[:, None, None]
    dh_part = (jnp.einsum('tkq,kpq->tkp', dy_slots, weights_down) * d_live[None, :, None]).astype(jnp.bfloat16)
    dh = column_sum(dh_part, d_rows, col_blocks)

    d_gate = (dh * up_saved * sig * (1.0 + gate_saved * (1.0 - sig))).astype(jnp.bfloat16)
    d_up = (dh * act).astype(jnp.bfloat16)
    grads = jnp.stack([d_gate, d_up]).reshape(2, TOKENS, col_blocks, BLOCK)[:, :, g_cols, :].astype(jnp.float32)
    grad_gu = jnp.einsum('tkp,gtkq->kgpq', x_slots, grads) * g_live[:, None, None, None]
    dx_part = (jnp.einsum('gtkq,kgpq->tkp', grads, weights_gu) * g_live[None, :, None]).astype(jnp.bfloat16)
    dx_saved = column_sum(dx_part, g_rows, row_blocks).astype(jnp.bfloat16)
    return (y_next, dx_saved, grad_gu.reshape(OWNERS, TILE_DEV, 2, BLOCK, BLOCK),
            grad_down.reshape(OWNERS, TILE_DEV, BLOCK, BLOCK))


def reference(x_next, x_saved, pending, gu_rows, gu_cols, gu_live, down_rows, down_cols, down_live, gate_up_tiles, down_tiles):
    results = []
    for section in range(SECTIONS):
        cot = pending[(section + 1) % SECTIONS]
        results.append(one_section(x_next[section], x_saved[section], cot, gu_rows[section], gu_cols[section], gu_live[section],
                                 down_rows[section], down_cols[section], down_live[section],
                                 gate_up_tiles[section], down_tiles[section]))
    return (jnp.stack([item[0] for item in results]), jnp.stack([item[1] for item in results]),
            jnp.stack([item[2] for item in results]), jnp.stack([item[3] for item in results]))
```

```python
import functools
import math

import jax
import jax.numpy as jnp
from jax import lax
from jax.experimental import pallas as pl
from jax.experimental.pallas import tpu as pltpu
from jax.sharding import PartitionSpec as P

F32 = jnp.float32
BF16 = jnp.bfloat16
I32 = jnp.int32


def dot(a, b, ca, cb):
    return lax.dot_general(a, b, (((ca,), (cb,)), ((), ())), preferred_element_type=F32)


def loop(count, body):
    def step(i, carry):
        body(i)
        return carry

    lax.fori_loop(0, count, step, 0)


def relay_kernel(
    n,
    pipes,
    side,
    g_rows,
    g_cols,
    g_live,
    d_rows,
    d_cols,
    d_live,
    gu_ref,
    dn_ref,
    xn_hbm,
    xs_hbm,
    pd_hbm,
    y_ref,
    dx_ref,
    ggu_ref,
    gdn_ref,
    xn,
    xs,
    pd,
    idx,
    gu_all,
    dn_all,
    cot_out,
    cot,
    xb,
    gate,
    up,
    hid,
    dh,
    dg,
    gu_give,
    gu_got,
    gu_own,
    gu_out,
    gu_in,
    dn_give,
    dn_got,
    dn_own,
    dn_out,
    dn_in,
    local_sem,
    idx_sem,
    gu_send,
    gu_recv,
    dn_send,
    dn_recv,
    cot_send,
    cot_recv,
    half_send,
    half_recv,
    full_send,
    full_recv,
):
    chips = n // 2
    tok = xn.shape[1]
    blk = dn_ref.shape[-1]
    me = lax.axis_index("tile")
    stage = lax.axis_index("pipe")
    core = me % 2
    chip = me // 2
    partner = chip * 2 + 1 - core
    chip_y, chip_x = chip // side, chip % side
    rows_of_chips = chips // side
    offsets = [(dy, dx) for dy in range(rows_of_chips) for dx in range(side)]
    offsets = sorted(offsets[1:], key=lambda o: -(o[0] + o[1]))
    peer_chips = [
        ((chip_y + dy) % rows_of_chips) * side + (chip_x + dx) % side for dy, dx in offsets
    ]
    peers = [c * 2 + core for c in peer_chips]
    nxt, prv = (stage + 1) % pipes, (stage + pipes - 1) % pipes

    def remote(src, dst, send, recv, **where):
        return pltpu.make_async_remote_copy(
            src_ref=src, dst_ref=dst, send_sem=send, recv_sem=recv, device_id=where
        )

    def fetch(hbm, buf, at):
        def piece(b):
            cols = pl.ds(pl.multiple_of(b * blk, blk), blk)
            pltpu.make_async_copy(hbm.at[:, cols], buf.at[b], local_sem.at[at]).start()

        loop(buf.shape[0], piece)

    barrier = pltpu.get_barrier_semaphore()
    for where in (nxt, prv):
        pl.semaphore_signal(barrier, inc=1, device_id={"pipe": where})
    for peer in peers + [partner]:
        pl.semaphore_signal(barrier, inc=1, device_id={"tile": peer})
    fetch(pd_hbm, pd, 0)
    pl.semaphore_wait(barrier, len(peers) + 3)

    idx_copy = remote(d_cols, idx, idx_sem.at[0], idx_sem.at[1], pipe=nxt)
    idx_copy.start()
    sends = []

    def start(copy):
        copy.start()
        sends.append(copy)

    for i, peer in enumerate(peers + [partner]):
        start(remote(gu_ref, gu_all.at[me], gu_send.at[i], gu_recv.at[me], tile=peer))
    for i, peer in enumerate(peers + [partner]):
        start(remote(dn_ref, dn_all.at[me], dn_send.at[i], dn_recv.at[me], tile=peer))
    fetch(xs_hbm, xs, 1)
    fetch(xn_hbm, xn, 2)
    gu_all[me] = gu_ref[...]
    dn_all[me] = dn_ref[...]

    order = [2 * c + 1 - core for c in range(chips)] + [2 * c + core for c in range(chips)]

    idx_copy.wait_recv()
    pltpu.make_async_copy(pd, pd, local_sem.at[0]).wait()
    for slot in order:
        cot_out[slot] = pd[idx[0, slot, 0]]
        start(
            remote(
                cot_out.at[slot], cot.at[slot], cot_send.at[slot], cot_recv.at[slot], pipe=prv
            )
        )

    pltpu.make_async_copy(xs, xs, local_sem.at[1]).wait()
    pltpu.make_async_copy(xn, xn, local_sem.at[2]).wait()

    def fill(k):
        row = g_rows[0, k, 0]
        xb[k, :tok] = xn[row]
        xb[k, tok:] = xs[row]

    loop(n, fill)
    hid[n] = jnp.zeros((2 * tok, blk), BF16)

    def project(j, first):
        live = (g_live[0, j] > 0).astype(F32)
        for g, acc in ((0, gate), (1, up)):
            part = (dot(xb[j], gu_all[j, g], 1, 0) * live).astype(BF16).astype(F32)

            def add(k):
                same = (g_cols[0, j, 0] == g_cols[0, k, 0]).astype(F32)
                if first:
                    acc[k] = part * same
                else:
                    acc[k] = acc[k] + part * same

            loop(n, add)

    def gu_arrival(o):
        remote(gu_ref, gu_all.at[o], gu_send.at[0], gu_recv.at[o], tile=partner).wait_recv()

    def dn_arrival(o):
        remote(dn_ref, dn_all.at[o], dn_send.at[0], dn_recv.at[o], tile=partner).wait_recv()

    project(me, True)
    gu_arrival(partner)
    project(partner, False)
    for i, peer in enumerate(peers):
        gu_arrival(peer)
        start(
            remote(
                gu_all.at[peer], gu_all.at[peer], gu_send.at[chips + i], gu_recv.at[peer],
                tile=partner,
            )
        )
        project(peer, False)
    for i, peer in enumerate(peers):
        dn_arrival(peer)
        start(
            remote(
                dn_all.at[peer], dn_all.at[peer], dn_send.at[chips + i], dn_recv.at[peer],
                tile=partner,
            )
        )
    for c in peer_chips:
        other = c * 2 + 1 - core
        gu_arrival(other)
        project(other, False)

    def activate(k):
        gn = gate[k, :tok]
        hid[k, :tok] = (gn * jax.nn.sigmoid(gn) * up[k, :tok]).astype(BF16)
        g = gate[k, tok:]
        u = up[k, tok:]
        sig = jax.nn.sigmoid(g)
        act = g * sig
        hid[k, tok:] = (act * u).astype(BF16)
        gate[k, tok:] = u * sig * (1.0 + g * (1.0 - sig))
        up[k, tok:] = act

    loop(n, activate)

    def hidden_slot(j):
        found = jnp.int32(n)
        for k in range(n):
            back = n - 1 - k
            same = (g_cols[0, back, 0] == d_rows[0, j, 0]).astype(I32)
            found = found + same * (back - found)
        return found

    dn_arrival(partner)
    for c in peer_chips:
        dn_arrival(c * 2 + 1 - core)

    def forward(j):
        live = (d_live[0, j] > 0).astype(F32)
        h = hid[hidden_slot(j), :tok]
        y_ref[j] = (dot(h, dn_all[j], 1, 0) * live).astype(BF16)

    loop(n, forward)

    def zero(k):
        dh[k] = jnp.zeros((tok, blk), F32)

    loop(n, zero)

    for at, slot in enumerate(order):
        c = at % chips
        live = (d_live[0, slot] > 0).astype(F32)
        remote(
            cot_out.at[slot], cot.at[slot], cot_send.at[slot], cot_recv.at[slot], pipe=nxt
        ).wait_recv()
        dy = cot[slot]
        part = (dot(dy, dn_all[slot], 1, 1) * live).astype(BF16).astype(F32)

        def add(k):
            same = (d_rows[0, slot, 0] == g_cols[0, k, 0]).astype(F32)
            dh[k] = dh[k] + part * same

        loop(n, add)
        term = dot(hid[hidden_slot(slot), tok:], dy, 0, 0) * live
        if at < chips:
            dn_give[c] = term.astype(BF16)
            start(
                remote(
                    dn_give.at[c], dn_got.at[c], half_send.at[0, c], half_recv.at[0, c],
                    tile=partner,
                )
            )
        else:
            dn_own[c] = term

    def grads(k):
        d = dh[k]
        dg[k, 0] = (d * gate[k, tok:]).astype(BF16)
        dg[k, 1] = (d * up[k, tok:]).astype(BF16)

    loop(n, grads)

    def gu_term(slot, g):
        live = (g_live[0, slot] > 0).astype(F32)
        return dot(xb[slot, tok:], dg[slot, g], 0, 0) * live

    for c in range(chips):
        slot = 2 * c + 1 - core
        for g in range(2):
            gu_give[c, g] = gu_term(slot, g).astype(BF16)
        start(
            remote(
                gu_give.at[c], gu_got.at[c], half_send.at[1, c], half_recv.at[1, c], tile=partner
            )
        )

    def half_arrival(kind, give, got, c):
        remote(
            give.at[c], got.at[c], half_send.at[kind, c], half_recv.at[kind, c], tile=partner
        ).wait_recv()

    for i, c in enumerate(peer_chips):
        half_arrival(0, dn_give, dn_got, c)
        dn_out[i] = (dn_own[c] + dn_got[c].astype(F32)).astype(BF16)
        start(
            remote(
                dn_out.at[i], dn_in.at[chip], full_send.at[0, i], full_recv.at[0, chip],
                tile=2 * c + core,
            )
        )
    for c in range(chips):
        for g in range(2):
            gu_own[c, g] = gu_term(2 * c + core, g)
    for i, c in enumerate(peer_chips):
        half_arrival(1, gu_give, gu_got, c)
        for g in range(2):
            gu_out[i, g] = (gu_own[c, g] + gu_got[c, g].astype(F32)).astype(BF16)
        start(
            remote(
                gu_out.at[i], gu_in.at[chip], full_send.at[1, i], full_recv.at[1, chip],
                tile=2 * c + core,
            )
        )

    def backward(k):
        live = (g_live[0, k] > 0).astype(F32)
        both = dot(dg[k, 0], gu_all[k, 0], 1, 1) + dot(dg[k, 1], gu_all[k, 1], 1, 1)
        dx_ref[k] = (both * live).astype(BF16)

    loop(n, backward)

    half_arrival(0, dn_give, dn_got, chip)
    half_arrival(1, gu_give, gu_got, chip)
    total_dn = dn_own[chip] + dn_got[chip].astype(F32)
    for c in peer_chips:
        remote(
            dn_out.at[0], dn_in.at[c], full_send.at[0, 0], full_recv.at[0, c], tile=partner
        ).wait_recv()
        total_dn = total_dn + dn_in[c].astype(F32)
    gdn_ref[...] = total_dn
    for c in peer_chips:
        remote(
            gu_out.at[0], gu_in.at[c], full_send.at[1, 0], full_recv.at[1, c], tile=partner
        ).wait_recv()
    for g in range(2):
        total = gu_own[chip, g] + gu_got[chip, g].astype(F32)
        for c in peer_chips:
            total = total + gu_in[c, g].astype(F32)
        ggu_ref[g] = total
    idx_copy.wait_send()
    for copy in sends:
        copy.wait_send()


def place_kernel(n, d_cols, g_rows, y_part, dx_part, y_hbm, dx_hbm, y_buf, dx_buf, sem):
    tok, blk = y_part.shape[1:]
    copies = []
    for at, (index, part, buf, hbm) in enumerate(
        ((d_cols, y_part, y_buf, y_hbm), (g_rows, dx_part, dx_buf, dx_hbm))
    ):
        buf[...] = jnp.zeros_like(buf)

        def put(j):
            def add(k, total):
                same = (index[0, k, 0] == index[0, j, 0]).astype(F32)
                return total + part[k].astype(F32) * same

            total = lax.fori_loop(0, n, add, jnp.zeros((tok, blk), F32))
            col = pl.multiple_of(index[0, j, 0] * blk, blk)
            buf[:, pl.ds(col, blk)] = total.astype(BF16)

        loop(n, put)
        copy = pltpu.make_async_copy(buf, hbm, sem.at[at])
        copy.start()
        copies.append(copy)
    for copy in copies:
        copy.wait()


def per_device(
    pipes,
    n,
    x_next,
    x_saved,
    pending,
    gu_rows,
    gu_cols,
    gu_live,
    down_rows,
    down_cols,
    down_live,
    gate_up_tiles,
    down_tiles,
):
    tok, width = x_next.shape[1:]
    blk = down_tiles.shape[-1]
    chips = n // 2
    side = math.isqrt(chips)
    if side * side != chips:
        side = 1
    smem = pl.BlockSpec(memory_space=pltpu.SMEM)
    vmem = pl.BlockSpec(memory_space=pltpu.VMEM)
    hbm = pl.BlockSpec(memory_space=pl.ANY)
    dma = pltpu.SemaphoreType.DMA
    y_part, dx_part, ggu, gdn = pl.pallas_call(
        functools.partial(relay_kernel, n, pipes, side),
        name="relay",
        out_shape=(
            jax.ShapeDtypeStruct((n, tok, blk), BF16),
            jax.ShapeDtypeStruct((n, tok, blk), BF16),
            jax.ShapeDtypeStruct((2, blk, blk), F32),
            jax.ShapeDtypeStruct((blk, blk), F32),
        ),
        in_specs=[smem] * 6 + [vmem] * 2 + [hbm] * 3,
        out_specs=(vmem, vmem, vmem, vmem),
        scratch_shapes=[
            pltpu.VMEM((width // blk, tok, blk), BF16),
            pltpu.VMEM((width // blk, tok, blk), BF16),
            pltpu.VMEM((width // blk, tok, blk), BF16),
            pltpu.SMEM((1, n, 1), I32),
            pltpu.VMEM((n, 2, blk, blk), BF16),
            pltpu.VMEM((n, blk, blk), BF16),
            pltpu.VMEM((n, tok, blk), BF16),
            pltpu.VMEM((n, tok, blk), BF16),
            pltpu.VMEM((n, 2 * tok, blk), BF16),
            pltpu.VMEM((n, 2 * tok, blk), F32),
            pltpu.VMEM((n, 2 * tok, blk), F32),
            pltpu.VMEM((n + 1, 2 * tok, blk), BF16),
            pltpu.VMEM((n, tok, blk), F32),
            pltpu.VMEM((n, 2, tok, blk), BF16),
            pltpu.VMEM((chips, 2, blk, blk), BF16),
            pltpu.VMEM((chips, 2, blk, blk), BF16),
            pltpu.VMEM((chips, 2, blk, blk), F32),
            pltpu.VMEM((chips, 2, blk, blk), BF16),
            pltpu.VMEM((chips, 2, blk, blk), BF16),
            pltpu.VMEM((chips, blk, blk), BF16),
            pltpu.VMEM((chips, blk, blk), BF16),
            pltpu.VMEM((chips, blk, blk), F32),
            pltpu.VMEM((chips, blk, blk), BF16),
            pltpu.VMEM((chips, blk, blk), BF16),
            dma((3,)),
            dma((2,)),
            dma((2 * chips,)),
            dma((n,)),
            dma((2 * chips,)),
            dma((n,)),
            dma((n,)),
            dma((n,)),
            dma((2, chips)),
            dma((2, chips)),
            dma((2, chips)),
            dma((2, chips)),
        ],
        compiler_params=pltpu.CompilerParams(
            collective_id=0, has_side_effects=True, vmem_limit_bytes=60 * 1024 * 1024
        ),
    )(
        gu_rows,
        gu_cols,
        gu_live,
        down_rows,
        down_cols,
        down_live,
        gate_up_tiles.reshape(2, blk, blk),
        down_tiles.reshape(blk, blk),
        x_next.reshape(tok, width),
        x_saved.reshape(tok, width),
        pending.reshape(tok, width),
    )
    y, dx = pl.pallas_call(
        functools.partial(place_kernel, n),
        name="place",
        out_shape=(
            jax.ShapeDtypeStruct((tok, width), BF16),
            jax.ShapeDtypeStruct((tok, width), BF16),
        ),
        in_specs=[smem] * 2 + [vmem] * 2,
        out_specs=(hbm, hbm),
        scratch_shapes=[
            pltpu.VMEM((tok, width), BF16),
            pltpu.VMEM((tok, width), BF16),
            dma((2,)),
        ],
        compiler_params=pltpu.CompilerParams(vmem_limit_bytes=32 * 1024 * 1024),
    )(down_cols, gu_rows, y_part, dx_part)
    return (
        y[None],
        dx[None],
        ggu.reshape(1, 1, 1, 2, blk, blk),
        gdn.reshape(1, 1, 1, blk, blk),
    )


def solution(mesh):
    tokens = P("pipe", "tile", None)
    lists = P("pipe", None, None)
    lives = P("pipe", None)
    gu_place = P("pipe", "tile", None, None, None, None)
    dn_place = P("pipe", "tile", None, None, None)
    return jax.shard_map(
        functools.partial(per_device, mesh.shape["pipe"], mesh.shape["tile"]),
        mesh=mesh,
        in_specs=(
            tokens, tokens, tokens, lists, lists, lives, lists, lists, lives, gu_place, dn_place,
        ),
        out_specs=(tokens, tokens, gu_place, dn_place),
        check_vma=False,
    )
```

```python
import functools
import math

import jax
import jax.numpy as jnp
from jax import lax
from jax.experimental import pallas as pl
from jax.experimental.pallas import tpu as pltpu
from jax.sharding import PartitionSpec as P

F32 = jnp.float32
BF16 = jnp.bfloat16
I32 = jnp.int32


def dot(a, b, ca, cb):
    return lax.dot_general(a, b, (((ca,), (cb,)), ((), ())), preferred_element_type=F32)


def loop(count, body):
    def step(i, carry):
        body(i)
        return carry

    lax.fori_loop(0, count, step, 0)


def each(count, body):
    if count <= 8:
        for i in range(count):
            body(i)
    else:
        loop(count, body)


def latest(keys, key, count, none):
    found = jnp.int32(none)
    for q in range(count):
        same = (keys[q] == key).astype(I32)
        found = found + same * (q - found)
    return found


def relay_kernel(
    n,
    pipes,
    side,
    g_rows,
    g_cols,
    g_live,
    d_rows,
    d_cols,
    d_live,
    gu_ref,
    dn_ref,
    xn_hbm,
    xs_hbm,
    pd_hbm,
    y_ref,
    dx_ref,
    ggu_ref,
    gdn_ref,
    xn,
    xs,
    pd,
    idx,
    gu_all,
    dn_all,
    cot_out,
    cot,
    xb,
    gate,
    up,
    slope,
    hid,
    dh,
    y_sum,
    dx_sum,
    dg,
    gu_give,
    gu_got,
    gu_own,
    gu_out,
    gu_in,
    dn_give,
    dn_got,
    dn_own,
    dn_out,
    dn_in,
    local_sem,
    idx_sem,
    gu_send,
    gu_recv,
    dn_send,
    dn_recv,
    cot_send,
    cot_recv,
    half_send,
    half_recv,
    full_send,
    full_recv,
):
    chips = n // 2
    tok = xn.shape[1]
    blk = dn_ref.shape[-1]
    me = lax.axis_index("tile")
    stage = lax.axis_index("pipe")
    core = me % 2
    chip = me // 2
    partner = chip * 2 + 1 - core
    chip_y, chip_x = chip // side, chip % side
    rows_of_chips = chips // side
    offsets = [(dy, dx) for dy in range(rows_of_chips) for dx in range(side)]
    offsets = sorted(offsets[1:], key=lambda o: -(o[0] + o[1]))
    peer_chips = [
        ((chip_y + dy) % rows_of_chips) * side + (chip_x + dx) % side for dy, dx in offsets
    ]
    peers = [c * 2 + core for c in peer_chips]
    nxt, prv = (stage + 1) % pipes, (stage + pipes - 1) % pipes

    def remote(src, dst, send, recv, **where):
        return pltpu.make_async_remote_copy(
            src_ref=src, dst_ref=dst, send_sem=send, recv_sem=recv, device_id=where
        )

    def fetch(hbm, buf, at):
        def piece(b):
            cols = pl.ds(pl.multiple_of(b * blk, blk), blk)
            pltpu.make_async_copy(hbm.at[:, cols], buf.at[b], local_sem.at[at]).start()

        loop(buf.shape[0], piece)

    barrier = pltpu.get_barrier_semaphore()
    for where in (nxt, prv):
        pl.semaphore_signal(barrier, inc=1, device_id={"pipe": where})
    for peer in peers + [partner]:
        pl.semaphore_signal(barrier, inc=1, device_id={"tile": peer})
    fetch(pd_hbm, pd, 0)
    pl.semaphore_wait(barrier, len(peers) + 3)

    idx_copy = remote(d_cols, idx, idx_sem.at[0], idx_sem.at[1], pipe=nxt)
    idx_copy.start()
    sends = []

    def start(copy):
        copy.start()
        sends.append(copy)

    for i, peer in enumerate(peers + [partner]):
        start(remote(gu_ref, gu_all.at[me], gu_send.at[i], gu_recv.at[me], tile=peer))
    for i, peer in enumerate(peers + [partner]):
        start(remote(dn_ref, dn_all.at[me], dn_send.at[i], dn_recv.at[me], tile=peer))
    fetch(xs_hbm, xs, 1)
    fetch(xn_hbm, xn, 2)
    own_tiles = [
        pltpu.make_async_copy(gu_ref, gu_all.at[me], local_sem.at[3]),
        pltpu.make_async_copy(dn_ref, dn_all.at[me], local_sem.at[4]),
    ]
    for copy in own_tiles:
        copy.start()

    order = [2 * c + 1 - core for c in range(chips)] + [2 * c + core for c in range(chips)]

    idx_copy.wait_recv()
    pltpu.make_async_copy(pd, pd, local_sem.at[0]).wait()
    for slot in order:
        cot_out[slot] = pd[idx[0, slot]]
        start(
            remote(
                cot_out.at[slot], cot.at[slot], cot_send.at[slot], cot_recv.at[slot], pipe=prv
            )
        )

    pltpu.make_async_copy(xs, xs, local_sem.at[1]).wait()
    pltpu.make_async_copy(xn, xn, local_sem.at[2]).wait()

    def fill(k):
        row = g_rows[0, k]
        xb[k, :tok] = xn[row]
        xb[k, tok:] = xs[row]

    each(n, fill)
    hid[n] = jnp.zeros((2 * tok, blk), BF16)
    gate[n] = jnp.zeros((2 * tok, blk), F32)
    up[n] = jnp.zeros((2 * tok, blk), F32)
    dh[n] = jnp.zeros((tok, blk), F32)
    y_sum[n] = jnp.zeros((tok, blk), F32)
    dx_sum[n] = jnp.zeros((tok, blk), F32)

    gu_order = [me, partner] + peers + [c * 2 + 1 - core for c in peer_chips]
    gu_keys = [g_cols[0, o] for o in gu_order]
    dn_keys = [d_rows[0, o] for o in order]
    g_keys = [g_cols[0, k] for k in range(n)]

    def project(p):
        j = gu_order[p]
        live = (g_live[0, j] > 0).astype(F32)
        tiles = jnp.concatenate([gu_all[j, 0], gu_all[j, 1]], axis=1)
        part = (dot(xb[j], tiles, 1, 0) * live).astype(BF16).astype(F32)
        before = latest(gu_keys, gu_keys[p], p, n)
        gate[p] = part[:, :blk] + gate[before]
        up[p] = part[:, blk:] + up[before]

    def gu_arrival(o):
        remote(gu_ref, gu_all.at[o], gu_send.at[0], gu_recv.at[o], tile=partner).wait_recv()

    def dn_arrival(o):
        remote(dn_ref, dn_all.at[o], dn_send.at[0], dn_recv.at[o], tile=partner).wait_recv()

    for copy in own_tiles:
        copy.wait()
    project(0)
    gu_arrival(partner)
    project(1)
    for i, peer in enumerate(peers):
        gu_arrival(peer)
        start(
            remote(
                gu_all.at[peer], gu_all.at[peer], gu_send.at[chips + i], gu_recv.at[peer],
                tile=partner,
            )
        )
        project(2 + i)
    for i, peer in enumerate(peers):
        dn_arrival(peer)
        start(
            remote(
                dn_all.at[peer], dn_all.at[peer], dn_send.at[chips + i], dn_recv.at[peer],
                tile=partner,
            )
        )
    for i, c in enumerate(peer_chips):
        gu_arrival(c * 2 + 1 - core)
        project(2 + len(peers) + i)

    def activate(k):
        at = latest(gu_keys, g_cols[0, k], n, n)
        g = gate[at]
        u = up[at]
        sig = jax.nn.sigmoid(g)
        act = g * sig
        hid[k] = (act * u).astype(BF16)
        g, u, sig, act = g[tok:], u[tok:], sig[tok:], act[tok:]
        slope[k, 0] = u * sig * (1.0 + g * (1.0 - sig))
        slope[k, 1] = act

    each(n, activate)

    def hidden_slot(j):
        return latest(g_keys, d_rows[0, j], n, n)

    dn_arrival(partner)
    for c in peer_chips:
        dn_arrival(c * 2 + 1 - core)

    y_keys = [d_cols[0, k] for k in range(n)]
    dx_keys = [g_rows[0, k] for k in range(n)]

    for j in range(n):
        live = (d_live[0, j] > 0).astype(F32)
        part = (dot(hid[hidden_slot(j), :tok], dn_all[j], 1, 0) * live).astype(BF16)
        total = part.astype(F32) + y_sum[latest(y_keys, y_keys[j], j, n)]
        y_sum[j] = total
        y_ref[j] = total.astype(BF16)

    for at, slot in enumerate(order):
        c = at % chips
        live = (d_live[0, slot] > 0).astype(F32)
        remote(
            cot_out.at[slot], cot.at[slot], cot_send.at[slot], cot_recv.at[slot], pipe=nxt
        ).wait_recv()
        dy = cot[slot]
        part = (dot(dy, dn_all[slot], 1, 1) * live).astype(BF16).astype(F32)

        dh[at] = part + dh[latest(dn_keys, dn_keys[at], at, n)]
        term = dot(hid[hidden_slot(slot), tok:], dy, 0, 0) * live
        if at < chips:
            dn_give[c] = term.astype(BF16)
            start(
                remote(
                    dn_give.at[c], dn_got.at[c], half_send.at[0, c], half_recv.at[0, c],
                    tile=partner,
                )
            )
        else:
            dn_own[c] = term

    def grads(k):
        d = dh[latest(dn_keys, g_cols[0, k], n, n)]
        dg[k] = jnp.concatenate(
            [(d * slope[k, 0]).astype(BF16), (d * slope[k, 1]).astype(BF16)], axis=1
        )

    each(n, grads)

    def gu_term(slot):
        live = (g_live[0, slot] > 0).astype(F32)
        return dot(xb[slot, tok:], dg[slot], 0, 0) * live

    for c in range(chips):
        slot = 2 * c + 1 - core
        gu_give[c] = gu_term(slot).astype(BF16)
        start(
            remote(
                gu_give.at[c], gu_got.at[c], half_send.at[1, c], half_recv.at[1, c], tile=partner
            )
        )

    def half_arrival(kind, give, got, c):
        remote(
            give.at[c], got.at[c], half_send.at[kind, c], half_recv.at[kind, c], tile=partner
        ).wait_recv()

    for i, c in enumerate(peer_chips):
        half_arrival(0, dn_give, dn_got, c)
        dn_out[i] = (dn_own[c] + dn_got[c].astype(F32)).astype(BF16)
        start(
            remote(
                dn_out.at[i], dn_in.at[chip], full_send.at[0, i], full_recv.at[0, chip],
                tile=2 * c + core,
            )
        )
    for c in range(chips):
        gu_own[c] = gu_term(2 * c + core)
    for i, c in enumerate(peer_chips):
        half_arrival(1, gu_give, gu_got, c)
        gu_out[i] = (gu_own[c] + gu_got[c].astype(F32)).astype(BF16)
        start(
            remote(
                gu_out.at[i], gu_in.at[chip], full_send.at[1, i], full_recv.at[1, chip],
                tile=2 * c + core,
            )
        )

    for k in range(n):
        live = (g_live[0, k] > 0).astype(F32)
        tiles = jnp.concatenate([gu_all[k, 0], gu_all[k, 1]], axis=1)
        part = (dot(dg[k], tiles, 1, 1) * live).astype(BF16)
        total = part.astype(F32) + dx_sum[latest(dx_keys, dx_keys[k], k, n)]
        dx_sum[k] = total
        dx_ref[k] = total.astype(BF16)

    half_arrival(0, dn_give, dn_got, chip)
    half_arrival(1, gu_give, gu_got, chip)
    total_dn = dn_own[chip] + dn_got[chip].astype(F32)
    for c in peer_chips:
        remote(
            dn_out.at[0], dn_in.at[c], full_send.at[0, 0], full_recv.at[0, c], tile=partner
        ).wait_recv()
        total_dn = total_dn + dn_in[c].astype(F32)
    gdn_ref[...] = total_dn
    for c in peer_chips:
        remote(
            gu_out.at[0], gu_in.at[c], full_send.at[1, 0], full_recv.at[1, c], tile=partner
        ).wait_recv()
    total = gu_own[chip] + gu_got[chip].astype(F32)
    for c in peer_chips:
        total = total + gu_in[c].astype(F32)
    ggu_ref[0] = total[:, :blk]
    ggu_ref[1] = total[:, blk:]
    idx_copy.wait_send()
    for copy in sends:
        copy.wait_send()


def place_kernel(
    n,
    d_cols,
    g_rows,
    y_part,
    dx_part,
    ggu,
    gdn,
    y_hbm,
    dx_hbm,
    ggu_hbm,
    gdn_hbm,
    y_buf,
    dx_buf,
    y_in,
    dx_in,
    ggu_in,
    gdn_in,
    in_sem,
    out_sem,
):
    blk = y_part.shape[-1]
    pairs = ((y_part, y_in), (dx_part, dx_in), (ggu, ggu_in), (gdn, gdn_in))
    reads = [pltpu.make_async_copy(a, b, in_sem.at[i]) for i, (a, b) in enumerate(pairs)]
    pairs = ((y_buf, y_hbm), (dx_buf, dx_hbm), (ggu_in, ggu_hbm), (gdn_in, gdn_hbm))
    writes = [pltpu.make_async_copy(a, b, out_sem.at[i]) for i, (a, b) in enumerate(pairs)]
    for read in reads:
        read.start()

    for at, (index, part, buf) in enumerate(((d_cols, y_in, y_buf), (g_rows, dx_in, dx_buf))):
        buf[...] = jnp.zeros_like(buf)
        reads[at].wait()

        def put(j):
            col = pl.multiple_of(index[0, j] * blk, blk)
            buf[:, pl.ds(col, blk)] = part[j]

        each(n, put)
        writes[at].start()
    for at in (2, 3):
        reads[at].wait()
        writes[at].start()
    for write in writes:
        write.wait()


def per_device(
    pipes,
    n,
    x_next,
    x_saved,
    pending,
    gu_rows,
    gu_cols,
    gu_live,
    down_rows,
    down_cols,
    down_live,
    gate_up_tiles,
    down_tiles,
):
    tok, width = x_next.shape[1:]
    blk = down_tiles.shape[-1]
    chips = n // 2
    side = math.isqrt(chips)
    if side * side != chips:
        side = 1
    smem = pl.BlockSpec(memory_space=pltpu.SMEM)
    vmem = pl.BlockSpec(memory_space=pltpu.VMEM)
    hbm = pl.BlockSpec(memory_space=pl.ANY)
    dma = pltpu.SemaphoreType.DMA
    y_part, dx_part, ggu, gdn = pl.pallas_call(
        functools.partial(relay_kernel, n, pipes, side),
        name="relay",
        out_shape=(
            jax.ShapeDtypeStruct((n, tok, blk), BF16),
            jax.ShapeDtypeStruct((n, tok, blk), BF16),
            jax.ShapeDtypeStruct((2, blk, blk), F32),
            jax.ShapeDtypeStruct((blk, blk), F32),
        ),
        in_specs=[smem] * 6 + [pl.BlockSpec(memory_space=pltpu.HBM)] * 5,
        out_specs=(vmem, vmem, vmem, vmem),
        scratch_shapes=[
            pltpu.VMEM((width // blk, tok, blk), BF16),
            pltpu.VMEM((width // blk, tok, blk), BF16),
            pltpu.VMEM((width // blk, tok, blk), BF16),
            pltpu.SMEM((1, n), I32),
            pltpu.VMEM((n, 2, blk, blk), BF16),
            pltpu.VMEM((n, blk, blk), BF16),
            pltpu.VMEM((n, tok, blk), BF16),
            pltpu.VMEM((n, tok, blk), BF16),
            pltpu.VMEM((n, 2 * tok, blk), BF16),
            pltpu.VMEM((n + 1, 2 * tok, blk), F32),
            pltpu.VMEM((n + 1, 2 * tok, blk), F32),
            pltpu.VMEM((n, 2, tok, blk), F32),
            pltpu.VMEM((n + 1, 2 * tok, blk), BF16),
            pltpu.VMEM((n + 1, tok, blk), F32),
            pltpu.VMEM((n + 1, tok, blk), F32),
            pltpu.VMEM((n + 1, tok, blk), F32),
            pltpu.VMEM((n, tok, 2 * blk), BF16),
            pltpu.VMEM((chips, blk, 2 * blk), BF16),
            pltpu.VMEM((chips, blk, 2 * blk), BF16),
            pltpu.VMEM((chips, blk, 2 * blk), F32),
            pltpu.VMEM((chips, blk, 2 * blk), BF16),
            pltpu.VMEM((chips, blk, 2 * blk), BF16),
            pltpu.VMEM((chips, blk, blk), BF16),
            pltpu.VMEM((chips, blk, blk), BF16),
            pltpu.VMEM((chips, blk, blk), F32),
            pltpu.VMEM((chips, blk, blk), BF16),
            pltpu.VMEM((chips, blk, blk), BF16),
            dma((5,)),
            dma((2,)),
            dma((2 * chips,)),
            dma((n,)),
            dma((2 * chips,)),
            dma((n,)),
            dma((n,)),
            dma((n,)),
            dma((2, chips)),
            dma((2, chips)),
            dma((2, chips)),
            dma((2, chips)),
        ],
        compiler_params=pltpu.CompilerParams(
            collective_id=0, has_side_effects=True, vmem_limit_bytes=62 << 20
        ),
    )(
        gu_rows.reshape(1, n),
        gu_cols.reshape(1, n),
        gu_live,
        down_rows.reshape(1, n),
        down_cols.reshape(1, n),
        down_live,
        gate_up_tiles.reshape(2, blk, blk),
        down_tiles.reshape(blk, blk),
        x_next.reshape(tok, width),
        x_saved.reshape(tok, width),
        pending.reshape(tok, width),
    )
    y, dx, ggu, gdn = pl.pallas_call(
        functools.partial(place_kernel, n),
        name="place",
        out_shape=(
            jax.ShapeDtypeStruct((tok, width), BF16),
            jax.ShapeDtypeStruct((tok, width), BF16),
            jax.ShapeDtypeStruct((2, blk, blk), F32),
            jax.ShapeDtypeStruct((blk, blk), F32),
        ),
        in_specs=[smem] * 2 + [hbm] * 4,
        out_specs=(hbm,) * 4,
        scratch_shapes=[
            pltpu.VMEM((tok, width), BF16),
            pltpu.VMEM((tok, width), BF16),
            pltpu.VMEM((n, tok, blk), BF16),
            pltpu.VMEM((n, tok, blk), BF16),
            pltpu.VMEM((2, blk, blk), F32),
            pltpu.VMEM((blk, blk), F32),
            dma((4,)),
            dma((4,)),
        ],
        compiler_params=pltpu.CompilerParams(vmem_limit_bytes=62 << 20),
    )(down_cols.reshape(1, n), gu_rows.reshape(1, n), y_part, dx_part, ggu, gdn)
    return (
        y[None],
        dx[None],
        ggu.reshape(1, 1, 1, 2, blk, blk),
        gdn.reshape(1, 1, 1, blk, blk),
    )


def solution(mesh):
    tokens = P("pipe", "tile", None)
    lists = P("pipe", None, None)
    lives = P("pipe", None)
    gu_place = P("pipe", "tile", None, None, None, None)
    dn_place = P("pipe", "tile", None, None, None)
    return jax.shard_map(
        functools.partial(per_device, mesh.shape["pipe"], mesh.shape["tile"]),
        mesh=mesh,
        in_specs=(
            tokens, tokens, tokens, lists, lists, lives, lists, lists, lives, gu_place, dn_place,
        ),
        out_specs=(tokens, tokens, gu_place, dn_place),
        check_vma=False,
    )
```

```python
import functools
import math

import jax
import jax.numpy as jnp
from jax import lax
from jax.experimental import pallas as pl
from jax.experimental.pallas import tpu as pltpu
from jax.sharding import PartitionSpec as P

F32 = jnp.float32
BF16 = jnp.bfloat16
I32 = jnp.int32


def dot(a, b, ca, cb):
    return lax.dot_general(a, b, (((ca,), (cb,)), ((), ())), preferred_element_type=F32)


def loop(count, body):
    def step(i, carry):
        body(i)
        return carry

    lax.fori_loop(0, count, step, 0)


def each(count, body):
    if count <= 8:
        for i in range(count):
            body(i)
    else:
        loop(count, body)


def latest(keys, key, count, none):
    found = jnp.int32(none)
    for q in range(count):
        same = (keys[q] == key).astype(I32)
        found = found + same * (q - found)
    return found


def relay_kernel(
    n,
    pipes,
    side,
    g_rows,
    g_cols,
    g_live,
    d_rows,
    d_cols,
    d_live,
    gu_ref,
    dn_ref,
    xn_hbm,
    xs_hbm,
    pd_hbm,
    y_ref,
    dx_ref,
    ggu_ref,
    gdn_ref,
    xn,
    xs,
    pd,
    idx,
    gu_all,
    dn_all,
    cot_out,
    cot,
    xb,
    gate,
    up,
    slope,
    hid,
    dh,
    y_sum,
    dx_sum,
    dg,
    gu_give,
    gu_got,
    gu_own,
    gu_out,
    gu_in,
    dn_give,
    dn_got,
    dn_own,
    dn_out,
    dn_in,
    local_sem,
    idx_sem,
    gu_send,
    gu_recv,
    dn_send,
    dn_recv,
    cot_send,
    cot_recv,
    half_send,
    half_recv,
    full_send,
    full_recv,
):
    chips = n // 2
    tok = xn.shape[1]
    blk = dn_ref.shape[-1]
    me = lax.axis_index("tile")
    stage = lax.axis_index("pipe")
    core = me % 2
    chip = me // 2
    partner = chip * 2 + 1 - core
    chip_y, chip_x = chip // side, chip % side
    rows_of_chips = chips // side
    offsets = [(dy, dx) for dy in range(rows_of_chips) for dx in range(side)]
    offsets = sorted(offsets[1:], key=lambda o: -(o[0] + o[1]))
    peer_chips = [
        ((chip_y + dy) % rows_of_chips) * side + (chip_x + dx) % side for dy, dx in offsets
    ]
    peers = [c * 2 + core for c in peer_chips]
    nxt, prv = (stage + 1) % pipes, (stage + pipes - 1) % pipes

    def remote(src, dst, send, recv, **where):
        return pltpu.make_async_remote_copy(
            src_ref=src, dst_ref=dst, send_sem=send, recv_sem=recv, device_id=where
        )

    def fetch(hbm, buf, at):
        for b in range(buf.shape[0]):
            cols = pl.ds(b * blk, blk)
            pltpu.make_async_copy(hbm.at[:, cols], buf.at[b], local_sem.at[at]).start()

    barrier = pltpu.get_barrier_semaphore()
    for where in (nxt, prv):
        pl.semaphore_signal(barrier, inc=1, device_id={"pipe": where})
    for peer in peers + [partner]:
        pl.semaphore_signal(barrier, inc=1, device_id={"tile": peer})
    fetch(pd_hbm, pd, 0)
    pl.semaphore_wait(barrier, len(peers) + 3)

    idx_copy = remote(d_cols, idx, idx_sem.at[0], idx_sem.at[1], pipe=nxt)
    idx_copy.start()
    sends = []

    def start(copy):
        copy.start()
        sends.append(copy)

    for i, peer in enumerate(peers + [partner]):
        start(remote(gu_ref, gu_all.at[me], gu_send.at[i], gu_recv.at[me], tile=peer))
    for i, peer in enumerate(peers + [partner]):
        start(remote(dn_ref, dn_all.at[me], dn_send.at[i], dn_recv.at[me], tile=peer))
    fetch(xs_hbm, xs, 1)
    fetch(xn_hbm, xn, 2)
    own_tiles = [
        pltpu.make_async_copy(gu_ref, gu_all.at[me], local_sem.at[3]),
        pltpu.make_async_copy(dn_ref, dn_all.at[me], local_sem.at[4]),
    ]
    for copy in own_tiles:
        copy.start()

    order = [2 * c + 1 - core for c in range(chips)] + [2 * c + core for c in range(chips)]

    idx_copy.wait_recv()
    pltpu.make_async_copy(pd, pd, local_sem.at[0]).wait()
    for slot in order:
        cot_out[slot] = pd[idx[0, slot]]
        start(
            remote(
                cot_out.at[slot], cot.at[slot], cot_send.at[slot], cot_recv.at[slot], pipe=prv
            )
        )

    pltpu.make_async_copy(xs, xs, local_sem.at[1]).wait()
    pltpu.make_async_copy(xn, xn, local_sem.at[2]).wait()

    def fill(k):
        row = g_rows[0, k]
        xb[k, :tok] = xn[row]
        xb[k, tok:] = xs[row]

    each(n, fill)
    hid[n] = jnp.zeros((2 * tok, blk), BF16)
    gate[n] = jnp.zeros((2 * tok, blk), F32)
    up[n] = jnp.zeros((2 * tok, blk), F32)
    dh[n] = jnp.zeros((tok, blk), F32)
    y_sum[n] = jnp.zeros((tok, blk), F32)
    dx_sum[n] = jnp.zeros((tok, blk), F32)

    gu_order = [me, partner] + peers + [c * 2 + 1 - core for c in peer_chips]
    gu_keys = [g_cols[0, o] for o in gu_order]
    dn_keys = [d_rows[0, o] for o in order]
    g_keys = [g_cols[0, k] for k in range(n)]

    def project(p):
        j = gu_order[p]
        live = (g_live[0, j] > 0).astype(F32)
        tiles = jnp.concatenate([gu_all[j, 0], gu_all[j, 1]], axis=1)
        part = (dot(xb[j], tiles, 1, 0) * live).astype(BF16).astype(F32)
        before = latest(gu_keys, gu_keys[p], p, n)
        gate[p] = part[:, :blk] + gate[before]
        up[p] = part[:, blk:] + up[before]

    def gu_arrival(o):
        remote(gu_ref, gu_all.at[o], gu_send.at[0], gu_recv.at[o], tile=partner).wait_recv()

    def dn_arrival(o):
        remote(dn_ref, dn_all.at[o], dn_send.at[0], dn_recv.at[o], tile=partner).wait_recv()

    for copy in own_tiles:
        copy.wait()
    project(0)
    gu_arrival(partner)
    project(1)
    for i, peer in enumerate(peers):
        gu_arrival(peer)
        start(
            remote(
                gu_all.at[peer], gu_all.at[peer], gu_send.at[chips + i], gu_recv.at[peer],
                tile=partner,
            )
        )
        project(2 + i)
    for i, peer in enumerate(peers):
        dn_arrival(peer)
        start(
            remote(
                dn_all.at[peer], dn_all.at[peer], dn_send.at[chips + i], dn_recv.at[peer],
                tile=partner,
            )
        )
    for i, c in enumerate(peer_chips):
        gu_arrival(c * 2 + 1 - core)
        project(2 + len(peers) + i)

    def activate(k):
        at = latest(gu_keys, g_cols[0, k], n, n)
        g = gate[at]
        u = up[at]
        sig = jax.nn.sigmoid(g)
        act = g * sig
        hid[k] = (act * u).astype(BF16)
        g, u, sig, act = g[tok:], u[tok:], sig[tok:], act[tok:]
        slope[k, 0] = u * sig * (1.0 + g * (1.0 - sig))
        slope[k, 1] = act

    each(n, activate)

    def hidden_slot(j):
        return latest(g_keys, d_rows[0, j], n, n)

    dn_arrival(partner)
    for c in peer_chips:
        dn_arrival(c * 2 + 1 - core)

    y_keys = [d_cols[0, k] for k in range(n)]
    dx_keys = [g_rows[0, k] for k in range(n)]

    for j in range(n):
        live = (d_live[0, j] > 0).astype(F32)
        part = (dot(hid[hidden_slot(j), :tok], dn_all[j], 1, 0) * live).astype(BF16)
        total = part.astype(F32) + y_sum[latest(y_keys, y_keys[j], j, n)]
        y_sum[j] = total
        y_ref[j] = total.astype(BF16)

    for at, slot in enumerate(order):
        c = at % chips
        live = (d_live[0, slot] > 0).astype(F32)
        remote(
            cot_out.at[slot], cot.at[slot], cot_send.at[slot], cot_recv.at[slot], pipe=nxt
        ).wait_recv()
        dy = cot[slot]
        part = (dot(dy, dn_all[slot], 1, 1) * live).astype(BF16).astype(F32)

        dh[at] = part + dh[latest(dn_keys, dn_keys[at], at, n)]
        term = dot(hid[hidden_slot(slot), tok:], dy, 0, 0) * live
        if at < chips:
            dn_give[c] = term.astype(BF16)
            start(
                remote(
                    dn_give.at[c], dn_got.at[c], half_send.at[0, c], half_recv.at[0, c],
                    tile=partner,
                )
            )
        else:
            dn_own[c] = term

    def grads(k):
        d = dh[latest(dn_keys, g_cols[0, k], n, n)]
        dg[k] = jnp.concatenate(
            [(d * slope[k, 0]).astype(BF16), (d * slope[k, 1]).astype(BF16)], axis=1
        )

    each(n, grads)

    def gu_term(slot):
        live = (g_live[0, slot] > 0).astype(F32)
        return dot(xb[slot, tok:], dg[slot], 0, 0) * live

    for c in peer_chips + [chip]:
        slot = 2 * c + 1 - core
        gu_give[c] = gu_term(slot).astype(BF16)
        start(
            remote(
                gu_give.at[c], gu_got.at[c], half_send.at[1, c], half_recv.at[1, c], tile=partner
            )
        )

    def half_arrival(kind, give, got, c):
        remote(
            give.at[c], got.at[c], half_send.at[kind, c], half_recv.at[kind, c], tile=partner
        ).wait_recv()

    for i, c in enumerate(peer_chips):
        half_arrival(0, dn_give, dn_got, c)
        dn_out[i] = (dn_own[c] + dn_got[c].astype(F32)).astype(BF16)
        start(
            remote(
                dn_out.at[i], dn_in.at[chip], full_send.at[0, i], full_recv.at[0, chip],
                tile=2 * c + core,
            )
        )
    for c in peer_chips + [chip]:
        gu_own[c] = gu_term(2 * c + core)
    for i, c in enumerate(peer_chips):
        half_arrival(1, gu_give, gu_got, c)
        gu_out[i] = (gu_own[c] + gu_got[c].astype(F32)).astype(BF16)
        start(
            remote(
                gu_out.at[i], gu_in.at[chip], full_send.at[1, i], full_recv.at[1, chip],
                tile=2 * c + core,
            )
        )

    for k in range(n):
        live = (g_live[0, k] > 0).astype(F32)
        tiles = jnp.concatenate([gu_all[k, 0], gu_all[k, 1]], axis=1)
        part = (dot(dg[k], tiles, 1, 1) * live).astype(BF16)
        total = part.astype(F32) + dx_sum[latest(dx_keys, dx_keys[k], k, n)]
        dx_sum[k] = total
        dx_ref[k] = total.astype(BF16)

    half_arrival(0, dn_give, dn_got, chip)
    half_arrival(1, gu_give, gu_got, chip)
    total_dn = dn_own[chip] + dn_got[chip].astype(F32)
    for c in peer_chips:
        remote(
            dn_out.at[0], dn_in.at[c], full_send.at[0, 0], full_recv.at[0, c], tile=partner
        ).wait_recv()
        total_dn = total_dn + dn_in[c].astype(F32)
    gdn_ref[...] = total_dn
    for c in peer_chips:
        remote(
            gu_out.at[0], gu_in.at[c], full_send.at[1, 0], full_recv.at[1, c], tile=partner
        ).wait_recv()
    total = gu_own[chip] + gu_got[chip].astype(F32)
    for c in peer_chips:
        total = total + gu_in[c].astype(F32)
    ggu_ref[0] = total[:, :blk]
    ggu_ref[1] = total[:, blk:]
    idx_copy.wait_send()
    for copy in sends:
        copy.wait_send()


def place_kernel(
    n,
    d_cols,
    g_rows,
    y_part,
    dx_part,
    ggu,
    gdn,
    y_hbm,
    dx_hbm,
    ggu_hbm,
    gdn_hbm,
    y_buf,
    dx_buf,
    y_in,
    dx_in,
    ggu_in,
    gdn_in,
    in_sem,
    out_sem,
):
    blk = y_part.shape[-1]
    pairs = ((y_part, y_in), (dx_part, dx_in), (ggu, ggu_in), (gdn, gdn_in))
    reads = [pltpu.make_async_copy(a, b, in_sem.at[i]) for i, (a, b) in enumerate(pairs)]
    pairs = ((y_buf, y_hbm), (dx_buf, dx_hbm), (ggu_in, ggu_hbm), (gdn_in, gdn_hbm))
    writes = [pltpu.make_async_copy(a, b, out_sem.at[i]) for i, (a, b) in enumerate(pairs)]
    for read in reads:
        read.start()

    for at, (index, part, buf) in enumerate(((d_cols, y_in, y_buf), (g_rows, dx_in, dx_buf))):
        buf[...] = jnp.zeros_like(buf)
        reads[at].wait()

        def put(j):
            col = pl.multiple_of(index[0, j] * blk, blk)
            buf[:, pl.ds(col, blk)] = part[j]

        each(n, put)
        writes[at].start()
    for at in (2, 3):
        reads[at].wait()
        writes[at].start()
    for write in writes:
        write.wait()


def per_device(
    pipes,
    n,
    x_next,
    x_saved,
    pending,
    gu_rows,
    gu_cols,
    gu_live,
    down_rows,
    down_cols,
    down_live,
    gate_up_tiles,
    down_tiles,
):
    tok, width = x_next.shape[1:]
    blk = down_tiles.shape[-1]
    chips = n // 2
    side = math.isqrt(chips)
    if side * side != chips:
        side = 1
    smem = pl.BlockSpec(memory_space=pltpu.SMEM)
    vmem = pl.BlockSpec(memory_space=pltpu.VMEM)
    hbm = pl.BlockSpec(memory_space=pl.ANY)
    dma = pltpu.SemaphoreType.DMA
    y_part, dx_part, ggu, gdn = pl.pallas_call(
        functools.partial(relay_kernel, n, pipes, side),
        name="relay",
        out_shape=(
            jax.ShapeDtypeStruct((n, tok, blk), BF16),
            jax.ShapeDtypeStruct((n, tok, blk), BF16),
            jax.ShapeDtypeStruct((2, blk, blk), F32),
            jax.ShapeDtypeStruct((blk, blk), F32),
        ),
        in_specs=[smem] * 6 + [pl.BlockSpec(memory_space=pltpu.HBM)] * 5,
        out_specs=(vmem, vmem, vmem, vmem),
        scratch_shapes=[
            pltpu.VMEM((width // blk, tok, blk), BF16),
            pltpu.VMEM((width // blk, tok, blk), BF16),
            pltpu.VMEM((width // blk, tok, blk), BF16),
            pltpu.SMEM((1, n), I32),
            pltpu.VMEM((n, 2, blk, blk), BF16),
            pltpu.VMEM((n, blk, blk), BF16),
            pltpu.VMEM((n, tok, blk), BF16),
            pltpu.VMEM((n, tok, blk), BF16),
            pltpu.VMEM((n, 2 * tok, blk), BF16),
            pltpu.VMEM((n + 1, 2 * tok, blk), F32),
            pltpu.VMEM((n + 1, 2 * tok, blk), F32),
            pltpu.VMEM((n, 2, tok, blk), F32),
            pltpu.VMEM((n + 1, 2 * tok, blk), BF16),
            pltpu.VMEM((n + 1, tok, blk), F32),
            pltpu.VMEM((n + 1, tok, blk), F32),
            pltpu.VMEM((n + 1, tok, blk), F32),
            pltpu.VMEM((n, tok, 2 * blk), BF16),
            pltpu.VMEM((chips, blk, 2 * blk), BF16),
            pltpu.VMEM((chips, blk, 2 * blk), BF16),
            pltpu.VMEM((chips, blk, 2 * blk), F32),
            pltpu.VMEM((chips, blk, 2 * blk), BF16),
            pltpu.VMEM((chips, blk, 2 * blk), BF16),
            pltpu.VMEM((chips, blk, blk), BF16),
            pltpu.VMEM((chips, blk, blk), BF16),
            pltpu.VMEM((chips, blk, blk), F32),
            pltpu.VMEM((chips, blk, blk), BF16),
            pltpu.VMEM((chips, blk, blk), BF16),
            dma((5,)),
            dma((2,)),
            dma((2 * chips,)),
            dma((n,)),
            dma((2 * chips,)),
            dma((n,)),
            dma((n,)),
            dma((n,)),
            dma((2, chips)),
            dma((2, chips)),
            dma((2, chips)),
            dma((2, chips)),
        ],
        compiler_params=pltpu.CompilerParams(
            collective_id=0, has_side_effects=True, vmem_limit_bytes=62 << 20
        ),
    )(
        gu_rows.reshape(1, n),
        gu_cols.reshape(1, n),
        gu_live,
        down_rows.reshape(1, n),
        down_cols.reshape(1, n),
        down_live,
        gate_up_tiles.reshape(2, blk, blk),
        down_tiles.reshape(blk, blk),
        x_next.reshape(tok, width),
        x_saved.reshape(tok, width),
        pending.reshape(tok, width),
    )
    y, dx, ggu, gdn = pl.pallas_call(
        functools.partial(place_kernel, n),
        name="place",
        out_shape=(
            jax.ShapeDtypeStruct((tok, width), BF16),
            jax.ShapeDtypeStruct((tok, width), BF16),
            jax.ShapeDtypeStruct((2, blk, blk), F32),
            jax.ShapeDtypeStruct((blk, blk), F32),
        ),
        in_specs=[smem] * 2 + [hbm] * 4,
        out_specs=(hbm,) * 4,
        scratch_shapes=[
            pltpu.VMEM((tok, width), BF16),
            pltpu.VMEM((tok, width), BF16),
            pltpu.VMEM((n, tok, blk), BF16),
            pltpu.VMEM((n, tok, blk), BF16),
            pltpu.VMEM((2, blk, blk), F32),
            pltpu.VMEM((blk, blk), F32),
            dma((4,)),
            dma((4,)),
        ],
        compiler_params=pltpu.CompilerParams(vmem_limit_bytes=62 << 20),
    )(down_cols.reshape(1, n), gu_rows.reshape(1, n), y_part, dx_part, ggu, gdn)
    return (
        y[None],
        dx[None],
        ggu.reshape(1, 1, 1, 2, blk, blk),
        gdn.reshape(1, 1, 1, blk, blk),
    )


def solution(mesh):
    tokens = P("pipe", "tile", None)
    lists = P("pipe", None, None)
    lives = P("pipe", None)
    gu_place = P("pipe", "tile", None, None, None, None)
    dn_place = P("pipe", "tile", None, None, None)
    return jax.shard_map(
        functools.partial(per_device, mesh.shape["pipe"], mesh.shape["tile"]),
        mesh=mesh,
        in_specs=(
            tokens, tokens, tokens, lists, lists, lives, lists, lists, lives, gu_place, dn_place,
        ),
        out_specs=(tokens, tokens, gu_place, dn_place),
        check_vma=False,
    )
```
